32 devices in a mesh: group: 4 (over z), leaf: 8 (over y, x, core).
Axes of the slice: x: 2, y: 2, z: 4, core: 2. Of those that a mesh axis runs over, the one named last changes fastest.
Arguments:
- observations: float32 [64, 32768], P(None, ('group', 'leaf')), may hold values from -6 to 6
- coordinates: float32 [3, 32768], P(None, ('group', 'leaf')), may hold values from 0 to 8, as said below
- proxies: float32 [32, 3, 64], P(('group', 'leaf')), may hold values from 0 to 8, as said below
- noise_variance: float32 [32768], P(('group', 'leaf')), may hold values from 0.5 to 2
- ordering: int32 [32, 1024], P(('group', 'leaf')), may hold values from 0 to 1023, each once within a row
- near_list: int32 [32, 7], P(('group', 'leaf')), may hold values from 0 to 31, as said below
- far_within: int32 [32, 6], P(('group', 'leaf')), may hold values from 0 to 7, as said below
- far_across: int32 [32, 3, 2], P(('group', 'leaf')), may hold values from 0 to 7, as said below
- couplings: bfloat16 [32, 12, 64, 64], P(('group', 'leaf')), may hold values from -0.4375 to 0.4375
Outputs:
- gain: float32 [64, 32768], P(None, ('group', 'leaf'))
- residual: float32 [64, 32768], P(None, ('group', 'leaf'))
The draws below stay inside these ranges and needn't reach their ends.
Inputs may be any that keep to these rules, and one draw needn't show every extreme that they name: `near_list`: row L names seven distinct leaves (L + d) mod 32 with d among -4, -3, -2, -1, 1, 2, 3, 4, in ascending order of d; the missing d is drawn for each leaf on its own and may be the same for different leaves. `far_within`: row L names 6 distinct leaves of L's own group by their index within the group, never L itself. `far_across`: entry [L, k, a] names, by its index within the group, a leaf of the group k + 1 places after L's own group, modulo the number of groups; the 2 entries of one [L, k] are distinct. Point coordinate 0 of leaf L lies in [L / 4, (L + 1) / 4]; coordinates 1 and 2 lie in [0, 8]. `proxies`: proxy coordinate 0 of leaf L lies in [L / 4, (L + 1) / 4]; coordinates 1 and 2 lie in [0, 8].
All inputs are finite; a program needn't handle non-finite values.
Results may differ from the reference program's by a relative error of at most 0.0045.
Values may be sent and summed in bfloat16 or wider, within the bound.
A program may use at most 128 MiB of HBM per device.

```python
import math
import jax
import jax.numpy as jnp
from jax import lax

LEAF_PTS = 1024
COLS = 64
RANK = 64
FW = 6
ACROSS = 2
ITERS = 2
LEAVES = 32
POINTS = 32768
FAR = 12
N_GROUP = 4
N_LEAF = 8


slab_width = 0.25


side_length = 8.0


neighbour_offsets = (-4, -3, -2, -1, 1, 2, 3, 4)


def place_points(key, leaf_ids, count):
    uniform = jax.random.uniform(key, (3, count), jnp.float32)
    across = uniform[1:]
    first = (leaf_ids.astype(jnp.float32) + uniform[0]) * slab_width
    return jnp.concatenate([first[None, :], across * side_length], axis=0)


def draw_coordinates(key, part):
    leaf_ids = jnp.arange(POINTS, dtype=jnp.int32) // LEAF_PTS
    return place_points(jax.random.fold_in(key, 11), leaf_ids, POINTS)


def draw_proxies(key, part):
    leaf_ids = jnp.arange(LEAVES * RANK, dtype=jnp.int32) // RANK
    placed = place_points(jax.random.fold_in(key, 13), leaf_ids, LEAVES * RANK)
    return placed.reshape(3, LEAVES, RANK).transpose(1, 0, 2)


def draw_near_list(key, part):
    offsets = jnp.array(neighbour_offsets, jnp.int32)
    dropped = jax.random.randint(jax.random.fold_in(key, 17), (LEAVES,), 0, 8)
    columns = jnp.arange(7, dtype=jnp.int32)[None, :]
    chosen = columns + (columns >= dropped[:, None]).astype(jnp.int32)
    leaf_ids = jnp.arange(LEAVES, dtype=jnp.int32)[:, None]
    return ((leaf_ids + offsets[chosen]) % LEAVES).astype(jnp.int32)


def draw_far_within(key, part):
    candidates = jnp.arange(N_LEAF, dtype=jnp.int32)
    scores = jax.random.randint(jax.random.fold_in(key, 19), (LEAVES, N_LEAF), 0, 1 << 20) * N_LEAF + candidates[None, :]
    own_place = jnp.arange(LEAVES, dtype=jnp.int32) % N_LEAF
    scores = jnp.where(candidates[None, :] == own_place[:, None], 1 << 30, scores)
    return jnp.argsort(scores, axis=1)[:, :FW].astype(jnp.int32)


def draw_far_across(key, part):
    candidates = jnp.arange(N_LEAF, dtype=jnp.int32)
    scores = jax.random.randint(jax.random.fold_in(key, 23), (LEAVES, N_GROUP - 1, N_LEAF), 0, 1 << 20) * N_LEAF + candidates[None, None, :]
    return jnp.argsort(scores, axis=2)[:, :, :ACROSS].astype(jnp.int32)


def level_of(rng, dims, pieces, least, high):
    level, own = 1.0, jax.random.fold_in(rng, 6)
    for axis_at, shards_of in pieces:
        heights = jnp.exp(jax.random.uniform(jax.random.fold_in(own, axis_at), (shards_of,), jnp.float32, least / len(pieces), high / len(pieces)))
        level = level * jnp.repeat(heights, dims[axis_at] // shards_of).reshape([-1 if axis == axis_at else 1 for axis in range(len(dims))])
    return level


def noise(rng, extent, deviation, bound, shards=(), kind=jnp.bfloat16):
    values = jax.random.normal(rng, extent, jnp.float32) * deviation
    if len(shards) > 0:
        values = level_of(rng, extent, shards, -0.22, 0.18) * values
    return jnp.clip(values, min=-bound, max=bound).astype(kind)


def setup_inputs(seed: int = 0) -> dict:
    splits = jax.random.split(jax.random.key(seed), 10)
    return {
        "observations": noise(splits[0], (COLS, POINTS), 1.0, 6.0, ((1, 32),), jnp.float32),
        "coordinates": draw_coordinates(jax.random.fold_in(splits[9], 71), 0),
        "proxies": draw_proxies(jax.random.fold_in(splits[9], 71), 0),
        "noise_variance": jnp.clip(jnp.exp(math.log(2.0) - 1.3862944 * jax.random.uniform(splits[3], (POINTS,), jnp.float32) ** level_of(splits[3], (POINTS,), ((0, 32),), -0.2, 0.2)), 0.5, 2.0),
        "ordering": jax.vmap(lambda own: jax.random.permutation(own, LEAF_PTS))(jax.random.split(splits[4], LEAVES)).reshape((LEAVES, LEAF_PTS)).astype(jnp.int32),
        "near_list": draw_near_list(jax.random.fold_in(splits[9], 71), 0),
        "far_within": draw_far_within(jax.random.fold_in(splits[9], 71), 0),
        "far_across": draw_far_across(jax.random.fold_in(splits[9], 71), 0),
        "couplings": noise(splits[8], (LEAVES, FAR, RANK, RANK), (RANK * FAR // 4) ** -0.5, 0.4375, ((0, 32),)),
    }


length_scale = 0.5
kernel_scale = 8.0
lower_bound = 0.5
upper_bound = 4.0

def kernel_tile(source, target):
    squared = (source[0][:, None] - target[0][None, :]) ** 2
    squared = squared + (source[1][:, None] - target[1][None, :]) ** 2
    squared = squared + (source[2][:, None] - target[2][None, :]) ** 2
    return jnp.exp(-jnp.sqrt(squared) / length_scale)

def far_sources(far_within, far_across):
    leaf_ids = jnp.arange(LEAVES, dtype=jnp.int32)
    group_ids = leaf_ids // N_LEAF
    within = group_ids[:, None] * N_LEAF + far_within
    places = jnp.arange(1, N_GROUP, dtype=jnp.int32)
    others = (group_ids[:, None] + places[None, :]) % N_GROUP
    across = others[:, :, None] * N_LEAF + far_across
    return jnp.concatenate([within, across.reshape(LEAVES, -1)], axis=1).astype(jnp.int32)

def apply_operator(field, coords, leaf_basis, noise_leaf, tile_sources, far_ids, couplings):
    rounded = field.astype(jnp.bfloat16)
    packed = jnp.einsum('lcp,lrp->lcr', rounded.astype(jnp.float32), leaf_basis.astype(jnp.float32)).astype(jnp.bfloat16)

    def one_leaf(leaf_index):

        def add_tile(running, source_leaf):
            kernel_block = kernel_tile(coords[source_leaf], coords[leaf_index]).astype(jnp.bfloat16)
            return (running + jnp.dot(rounded[source_leaf], kernel_block, preferred_element_type=jnp.float32), None)
        near_part, _ = lax.scan(add_tile, jnp.zeros((COLS, LEAF_PTS), jnp.float32), tile_sources[leaf_index])
        listed = packed[far_ids[leaf_index]].astype(jnp.float32)
        spread = jnp.einsum('fcs,frs->cr', listed, couplings[leaf_index].astype(jnp.float32)).astype(jnp.bfloat16)
        far_part = jnp.dot(spread, leaf_basis[leaf_index], preferred_element_type=jnp.float32)
        return near_part + far_part
    kernel_part = lax.map(one_leaf, jnp.arange(LEAVES, dtype=jnp.int32))
    return noise_leaf * field + kernel_part / kernel_scale

def place_back(values, ordering):

    def one_leaf(block, point_order):
        return jnp.zeros_like(block).at[:, point_order].set(block)
    return jax.vmap(one_leaf)(values, ordering)

def reference(observations, coordinates, proxies, noise_variance, ordering, near_list, far_within, far_across, couplings):
    coords = coordinates.reshape(3, LEAVES, LEAF_PTS).transpose(1, 0, 2)
    sensor_values = observations.reshape(COLS, LEAVES, LEAF_PTS).transpose(1, 0, 2)
    right_side = jnp.take_along_axis(sensor_values, ordering[:, None, :], axis=2)
    noise_leaf = jnp.take_along_axis(noise_variance.reshape(LEAVES, LEAF_PTS), ordering, axis=1)[:, None, :]
    leaf_basis = jax.vmap(kernel_tile)(proxies, coords).astype(jnp.bfloat16)
    tile_sources = jnp.concatenate([jnp.arange(LEAVES, dtype=jnp.int32)[:, None], near_list], axis=1).astype(jnp.int32)
    far_ids = far_sources(far_within, far_across)
    centre = (upper_bound + lower_bound) / 2.0
    half_width = (upper_bound - lower_bound) / 2.0
    ratio_now = 1.0 / (centre / half_width)
    solution = jnp.zeros_like(right_side)
    residual_field = right_side
    direction = right_side / centre
    for iteration in range(ITERS):
        solution = solution + direction
        residual_field = residual_field - apply_operator(direction, coords, leaf_basis, noise_leaf, tile_sources, far_ids, couplings)
        if iteration + 1 < ITERS:
            ratio_next = 1.0 / (2.0 * centre / half_width - ratio_now)
            direction = ratio_next * ratio_now * direction + 2.0 * ratio_next / half_width * residual_field
            ratio_now = ratio_next
    gain = place_back(solution, ordering).transpose(1, 0, 2).reshape(COLS, POINTS)
    residual = place_back(residual_field, ordering).transpose(1, 0, 2).reshape(COLS, POINTS)
    return (gain, residual)
```

```python
import functools
import math

import jax
import jax.numpy as jnp
from jax import lax
from jax.experimental import pallas as pl
from jax.experimental.pallas import tpu as pltpu
from jax.sharding import PartitionSpec as P

length_scale = 0.5
kernel_scale = 8.0
lower_bound = 0.5
upper_bound = 4.0
REACH = 4
SPAN = 2 * REACH + 1
SLAB = 0.25
SIDE = 8.0
SCALE = 1.0 / (length_scale * math.log(2.0))
TINY = 1e-12
BLOCK = 256
ROWS = 8
DEPTH = 128
RELAYED = ()
VMEM_LIMIT = 56 << 20
MESH = pl.DeviceIdType.MESH
F32 = jnp.float32
BF16 = jnp.bfloat16

LAST = (((1,), (1,)), ((), ()))


def dot(a, b):
    return jnp.dot(a, b, preferred_element_type=F32)


def dot_last(a, b):
    return lax.dot_general(a, b, LAST, preferred_element_type=F32)


def split3(x):
    high = x.astype(BF16).astype(F32)
    rest = x - high
    mid = rest.astype(BF16).astype(F32)
    low = (rest - mid).astype(BF16).astype(F32)
    return high, mid, low


def eight(coords):
    return jnp.concatenate(
        [coords, jnp.zeros((ROWS - coords.shape[0], coords.shape[1]), F32)], axis=0
    )


def features(coords, shift0):
    row = lax.broadcasted_iota(jnp.int32, coords.shape, 0)
    shift = jnp.where(row == 0, shift0, SIDE / 2)
    x = jnp.where(row < 3, (coords - shift) * SCALE, 0.0)
    h, m, l = split3(x)
    n1, n2, n3 = split3(jnp.sum(x * x, axis=0, keepdims=True))
    one = jnp.ones_like(x)
    zero = jnp.zeros_like(x)
    left = jnp.where(row == 0, n1, jnp.where(row == 1, n2, n3))
    left = jnp.where(row < 3, left, jnp.where(row < 6, one, zero))
    right = jnp.where(row == 3, n1, jnp.where(row == 4, n2, n3))
    right = jnp.where(row < 3, one, jnp.where(row < 6, right, zero))
    pad = [zero] * (DEPTH // ROWS - 10)
    source = jnp.concatenate([h, h, h, m, m, m, l, l, l, left] + pad, axis=0)
    h2, m2, l2 = -2.0 * h, -2.0 * m, -2.0 * l
    target = jnp.concatenate([h2, m2, l2, h2, m2, l2, h2, m2, l2, right] + pad, axis=0)
    return source, target


def from_squares(s):
    s = jnp.maximum(s, TINY)
    return jnp.exp2(-(s * lax.rsqrt(s))).astype(BF16)


def kernel(
    n_group,
    n_leaf,
    obs_hbm,
    coords_hbm,
    prox_hbm,
    noise_hbm,
    order_hbm,
    near_hbm,
    within_hbm,
    across_hbm,
    coup_hbm,
    gain_ref,
    resid_ref,
    obs_ref,
    coords_ref,
    prox_ref,
    noise_ref,
    order_ref,
    near_ref,
    within_ref,
    across_ref,
    coup_ref,
    cbuf,
    fld0,
    fld1,
    packed,
    tiles,
    ft,
    g_own,
    basis,
    acc,
    r1_ref,
    spread_ref,
    in_sem,
    c_send,
    c_recv,
    f_send,
    f_recv,
    z_send,
    z_recv,
    p_send,
    p_recv,
):
    leaves = n_group * n_leaf
    chips = leaves // 2
    cols, pts = obs_ref.shape
    blocks = pts // BLOCK
    halves = 2
    group = lax.axis_index("group")
    leaf = lax.axis_index("leaf")
    me = group * n_leaf + leaf
    odd = lax.rem(me, 2)
    delta = 1 - 2 * odd
    place_in_four = lax.rem(me // 2, 4)
    ex = 2 * (1 - 2 * lax.rem(place_in_four, 2))
    ey = 4 * (1 - 2 * (place_in_four // 2))

    def place(index):
        return (index // n_leaf, lax.rem(index, n_leaf))

    def at_offset(k):
        return place(lax.rem(me + k + leaves, leaves))

    partner = place(me + delta)

    barrier = pltpu.get_barrier_semaphore()
    near_offsets = [k for k in range(-REACH, REACH + 1) if k != 0]
    peers = [at_offset(k) for k in near_offsets if k % 2]
    peers += [at_offset(2 * t) for t in range(1, chips)]
    for peer in peers:
        pl.semaphore_signal(barrier, inc=1, device_id=peer, device_id_type=MESH)

    loads = [
        pltpu.make_async_copy(source, target, in_sem.at[n])
        for n, (source, target) in enumerate(
            (
                (order_hbm, order_ref),
                (coords_hbm, coords_ref),
                (obs_hbm, obs_ref),
                (prox_hbm, prox_ref),
                (near_hbm, near_ref),
                (within_hbm, within_ref),
                (across_hbm, across_ref),
                (noise_hbm, noise_ref),
                (coup_hbm, coup_ref),
            )
        )
    ]
    for c in loads:
        c.start()

    def remote(source, target, send, recv, device):
        return pltpu.make_async_remote_copy(
            src_ref=source,
            dst_ref=target,
            send_sem=send,
            recv_sem=recv,
            device_id=device,
            device_id_type=MESH,
        )

    def coord_copy(n, source, target, device):
        return remote(cbuf.at[source], cbuf.at[target], c_send.at[n], c_recv.at[n], device)

    coord_out = [
        coord_copy(n, REACH, REACH - k, at_offset(k)) for n, k in enumerate(near_offsets)
    ]
    coord_order = sorted(range(len(near_offsets)), key=lambda n: -abs(near_offsets[n]))

    class Exchange:
        def __init__(self, view, send, recv, relayed):
            def copy(source, target, which, device):
                return remote(
                    view(source), view(target), send.at[which], recv.at[which], device
                )

            self.relayed = relayed
            self.y = copy(REACH, REACH - ey, 1, at_offset(ey))
            self.x = copy(REACH, REACH - ex, 0, at_offset(ex))
            self.b = copy(REACH, REACH + ex, 2, at_offset(-ex))
            if relayed:
                self.a = copy(REACH + ey, REACH - ey, 3, at_offset(2 * ey))
            else:
                self.a = copy(REACH, REACH + ey, 3, at_offset(-ey))
            self.own = copy(REACH, REACH - delta, 4, partner)
            moved = (ex, -ex, 4 * delta)
            self.on = [
                copy(REACH + e, REACH + e - delta, 5 + n, partner)
                for n, e in enumerate(moved)
            ]
            back = (ex, -ex, -4 * delta)
            self.arriving = [copy(REACH, REACH + delta, 4, partner)] + [
                copy(REACH, REACH + e + delta, 5 + n, partner) for n, e in enumerate(back)
            ]

        def start(self):
            self.y.start()
            if not self.relayed:
                self.a.start()

        def start_rest(self):
            self.x.start()
            self.b.start()
            self.own.start()

        def relay(self):
            self.y.wait_recv()
            if self.relayed:
                self.a.start()

        def forward_x(self):
            self.x.wait_recv()
            self.on[0].start()

        def forward_b(self):
            self.b.wait_recv()
            self.on[1].start()

        def forward_a(self):
            self.a.wait_recv()
            self.on[2].start()

        def finish(self):
            for c in self.arriving:
                c.wait_recv()

        def drain(self):
            for c in [self.y, self.x, self.b, self.a, self.own] + self.on:
                c.wait_send()

    span = blocks // halves

    def half_view(h):
        return lambda slot: fld0.at[slot, pl.ds(h * span, span)]

    def block_view(b):
        return lambda slot: fld1[b].at[slot]

    field0 = [
        Exchange(half_view(h), f_send.at[h], f_recv.at[h], True) for h in range(halves)
    ]
    field1 = [
        Exchange(block_view(b), f_send.at[halves + b], f_recv.at[halves + b], b in RELAYED)
        for b in range(blocks)
    ]

    class Far:
        def __init__(self, it):
            def block(index):
                return packed[it].at[lax.rem(index, n_leaf), index // n_leaf]

            def shifted(t):
                return lax.rem(me + 2 * t, leaves)

            self.out = [
                remote(block(me), block(me), z_send.at[it, t], z_recv.at[it, t], place(shifted(t)))
                for t in range(1, chips)
            ]
            def slab(source, which):
                return remote(
                    packed[it].at[source],
                    packed[it].at[source],
                    p_send.at[it, which],
                    p_recv.at[it, which],
                    partner,
                )

            own = [lax.rem(leaf + 2 * t, n_leaf) for t in range(n_leaf // 2)]
            self.on = [slab(o, t) for t, o in enumerate(own)]
            self.last = [slab(o + delta, t) for t, o in enumerate(own)]

        def start(self):
            for c in self.out:
                c.start()

        def forward(self):
            for c in self.out:
                c.wait_recv()
            for c in self.on:
                c.start()

        def finish(self):
            for c in self.last:
                c.wait_recv()

        def drain(self):
            for c in self.out + self.on:
                c.wait_send()

    far0, far1 = Far(0), Far(1)

    loads[0].wait()
    loads[1].wait()
    slot_row = lax.broadcasted_iota(jnp.int32, (pts, pts), 0)
    pick = jnp.where(slot_row == order_ref[...], 1.0, 0.0).astype(BF16)
    raw = eight(coords_ref[...])
    pieces = jnp.concatenate(list(split3(raw)), axis=0).astype(BF16)
    moved = dot_last(pieces, pick)
    mine = (moved[:ROWS] + moved[ROWS : 2 * ROWS]) + moved[2 * ROWS :]
    cbuf[REACH] = mine[:3]

    centre = (upper_bound + lower_bound) / 2.0
    half_width = (upper_bound - lower_bound) / 2.0
    ratio0 = 1.0 / (centre / half_width)
    ratio1 = 1.0 / (2.0 * centre / half_width - ratio0)

    def block_of(b):
        return slice(b * BLOCK, (b + 1) * BLOCK)

    loads[2].wait()
    for b in range(blocks):
        fld0[REACH, b] = (obs_ref[:, block_of(b)] / centre).astype(BF16)
    pl.semaphore_wait(barrier, len(peers))
    for n in coord_order:
        coord_out[n].start()
    for h in range(halves):
        field0[h].start()

    shift0 = (me.astype(F32) + 0.5) * SLAB
    source, target = features(mine, shift0)
    g_own[...] = target.astype(BF16)
    ft[0] = source.T.astype(BF16)
    for c in loads[3:]:
        c.wait()
    rank = prox_ref.shape[2]
    prox = eight(jnp.concatenate([prox_ref[r] for r in range(3)], axis=0))
    prox = jnp.concatenate([prox, jnp.zeros((ROWS, 128 - rank), F32)], axis=1)
    prox_source, _ = features(prox, shift0)
    prox_t = prox_source.T.astype(BF16)[:rank]
    basis[...] = from_squares(dot(prox_t, g_own[...]))

    def field(it, slot, b):
        return fld0[slot, b] if it == 0 else fld1[b][slot]

    def pack(it):
        total = None
        for b in range(blocks):
            part = dot_last(field(it, REACH, b), basis[:, block_of(b)])
            total = part if total is None else total + part
        half = cols // 2
        packed[it][leaf, group] = jnp.concatenate(
            [total[:half], total[half:]], axis=1
        ).astype(BF16)

    pack(0)
    far0.start()
    for h in range(halves):
        field0[h].start_rest()

    def build(j, b, diagonal, slot=None):
        right = g_own[:, block_of(b)]
        total = None
        for c in range(pts // BLOCK):
            rows = slice(c * BLOCK, (c + 1) * BLOCK)
            s = dot(ft[j, rows, :], right)
            if diagonal and c == b:
                at = lax.broadcasted_iota(jnp.int32, s.shape, 0)
                to = lax.broadcasted_iota(jnp.int32, s.shape, 1)
                s = jnp.where(at == to, 0.0, s)
            tile = from_squares(s)
            tiles[j, b, rows, :] = tile
            if slot is not None:
                part = dot(field(0, slot, c), tile)
                total = part if total is None else total + part
        return total

    for b in range(blocks):
        build(0, b, True)

    for n in coord_order:
        coord_out[n].wait_recv()
    near_count = near_ref.shape[1]

    def slot_of(j):
        return jnp.minimum(lax.rem(near_ref[0, j] - me + REACH + leaves, leaves), SPAN - 1)

    def stack(j, carry):
        source, _ = features(eight(cbuf[slot_of(j)]), shift0)
        ft[j + 1] = source.T.astype(BF16)
        return carry

    lax.fori_loop(0, near_count, stack, 0)

    def build_near(b, after):
        for j in range(near_count):
            build(j + 1, b, False)
            for act in after.get(j, ()):
                act()

    def build_apply(b, after):
        total = term(0, b, range(blocks), REACH, 0)
        for j in range(near_count):
            total = total + build(j + 1, b, False, slot_of(j))
            for act in after.get(j, ()):
                act()
        return total

    def term(it, b, ks, slot, j):
        total = None
        for k in ks:
            part = dot(field(it, slot, k), tiles[j, b, k * BLOCK : (k + 1) * BLOCK, :])
            total = part if total is None else total + part
        return total

    def near(it, b, ks):
        total = term(it, b, ks, REACH, 0)
        for j in range(near_count):
            total = total + term(it, b, ks, slot_of(j), j + 1)
        return total

    def spread(it):
        total = None
        n_within = within_ref.shape[1]
        n_across = across_ref.shape[0]
        for f in range(coup_ref.shape[0]):
            if f < n_within:
                block = packed[it][within_ref[0, f], group]
            else:
                k, a = divmod(f - n_within, n_across)
                block = packed[it][across_ref[a, k], lax.rem(group + 1 + k, n_group)]
            block = jnp.concatenate([block[:, :rank], block[:, rank:]], axis=0)
            part = dot_last(block, coup_ref[f])
            total = part if total is None else total + part
        spread_ref[...] = total.astype(BF16)

    def step0(b, total):
        cut = block_of(b)
        near_part = total + dot(spread_ref[...], basis[:, cut])
        obs = obs_ref[:, cut]
        d0 = obs / centre
        res = obs - (noise_ref[:, cut] * d0 + near_part / kernel_scale)
        d1 = ratio1 * ratio0 * d0 + 2.0 * ratio1 / half_width * res
        fld1[b][REACH] = d1.astype(BF16)
        if b < blocks - 1:
            field1[b].start()
            field1[b].start_rest()
        r1_ref[:, cut] = res - noise_ref[:, cut] * d1
        gain_ref[:, cut] = d0 + d1

    def near_early(b, count):
        total = term(0, b, range(blocks), REACH, 0)
        for j in range(count):
            total = total + term(0, b, range(blocks), slot_of(j), j + 1)
        return total

    f0, f1 = field0
    build_near(0, {4: (f0.relay,)})
    f1.relay()
    build_near(1, {1: (f0.forward_x, f1.forward_x)})
    build_near(2, {1: (far0.forward,), 4: (f0.forward_b, f1.forward_b)})
    last = blocks - 1
    early = 3
    for j in range(early):
        build(j + 1, last, False)
        if j == 0:
            f0.forward_a()
            f1.forward_a()
    far0.finish()
    spread(0)
    f0.finish()
    f1.finish()
    for b in range(blocks - 1):
        step0(b, near(0, b, range(blocks)))
    total = near_early(last, early)
    acts = {3: (field1[0].relay,), 5: (field1[1].relay,)}
    for j in range(early, near_count):
        total = total + build(j + 1, last, False, slot_of(j))
        for act in acts.get(j, ()):
            act()
    for j in acts:
        if j < early:
            for act in acts[j]:
                act()
    step0(last, total)
    field1[3].start()
    field1[3].start_rest()
    pack(1)
    far1.start()
    field1[2].relay()
    for b in range(blocks):
        acc[:, block_of(b)] = term(1, b, range(blocks), REACH, 0)
    for e in field1[:2]:
        e.forward_x()
        e.forward_b()
    field1[0].forward_a()

    def late(ks):
        for b in range(blocks):
            cut = block_of(b)
            total = acc[:, cut]
            for j in range(near_count):
                total = total + term(1, b, ks, slot_of(j), j + 1)
            acc[:, cut] = total

    field1[1].forward_a()
    field1[0].finish()
    late((0,))
    field1[2].forward_x()
    field1[2].forward_b()
    field1[2].forward_a()
    field1[1].finish()
    late((1,))
    field1[3].relay()
    field1[3].forward_x()
    field1[3].forward_b()
    field1[3].forward_a()
    field1[2].finish()
    late((2,))
    far1.forward()
    field1[3].finish()
    late((3,))
    far1.finish()
    spread(1)

    for b in range(blocks):
        cut = block_of(b)
        total = acc[:, cut] + dot(spread_ref[...], basis[:, cut])
        resid_ref[:, cut] = r1_ref[:, cut] - total / kernel_scale

    for c in coord_out:
        c.wait_send()
    for e in field0 + field1:
        e.drain()
    far0.drain()
    far1.drain()


def local(
    n_group,
    n_leaf,
    observations,
    coordinates,
    proxies,
    noise_variance,
    ordering,
    near_list,
    far_within,
    far_across,
    couplings,
):
    operands = (
        observations,
        coordinates,
        jnp.transpose(proxies, (1, 0, 2)),
        noise_variance[None, :],
        ordering,
        near_list,
        far_within,
        jnp.transpose(far_across[0]),
        couplings[0],
    )
    cols, pts = observations.shape
    rank = proxies.shape[2]
    blocks = pts // BLOCK
    chips = n_group * n_leaf // 2
    vmem = pl.BlockSpec(memory_space=pltpu.VMEM)
    dma = pltpu.SemaphoreType.DMA
    spaces = [pltpu.VMEM] * 5 + [pltpu.SMEM] * 3 + [pltpu.VMEM]
    return pl.pallas_call(
        functools.partial(kernel, n_group, n_leaf),
        out_shape=(
            jax.ShapeDtypeStruct((cols, pts), F32),
            jax.ShapeDtypeStruct((cols, pts), F32),
        ),
        in_specs=[pl.BlockSpec(memory_space=pltpu.HBM)] * len(operands),
        out_specs=(vmem, vmem),
        scratch_shapes=[space(x.shape, x.dtype) for space, x in zip(spaces, operands)]
        + [
            pltpu.VMEM((SPAN, 3, pts), F32),
            pltpu.VMEM((SPAN, blocks, cols, BLOCK), BF16),
            [pltpu.VMEM((SPAN, cols, BLOCK), BF16)] * blocks,
            [pltpu.VMEM((n_leaf, n_group, cols // 2, 2 * rank), BF16)] * 2,
            pltpu.VMEM((near_list.shape[1] + 1, blocks, pts, BLOCK), BF16),
            pltpu.VMEM((near_list.shape[1] + 1, pts, DEPTH), BF16),
            pltpu.VMEM((DEPTH, pts), BF16),
            pltpu.VMEM((rank, pts), BF16),
            pltpu.VMEM((cols, pts), F32),
            pltpu.VMEM((cols, pts), F32),
            pltpu.VMEM((cols, rank), BF16),
            dma((len(operands),)),
            dma((8,)),
            dma((8,)),
            dma((2 + blocks, 8)),
            dma((2 + blocks, 8)),
            dma((2, chips)),
            dma((2, chips)),
            dma((2, n_leaf // 2)),
            dma((2, n_leaf // 2)),
        ],
        compiler_params=pltpu.CompilerParams(
            collective_id=0, has_side_effects=True, vmem_limit_bytes=VMEM_LIMIT
        ),
    )(*operands)


def solution(mesh):
    placed = (
        P(None, ("group", "leaf")),
        P(None, ("group", "leaf")),
        P(("group", "leaf"), None, None),
        P(("group", "leaf")),
        P(("group", "leaf"), None),
        P(("group", "leaf"), None),
        P(("group", "leaf"), None),
        P(("group", "leaf"), None, None),
        P(("group", "leaf"), None, None, None),
    )
    return jax.shard_map(
        functools.partial(local, mesh.shape["group"], mesh.shape["leaf"]),
        mesh=mesh,
        in_specs=placed,
        out_specs=(P(None, ("group", "leaf")), P(None, ("group", "leaf"))),
        check_vma=False,
    )
```
